32 devices in a mesh: dom: 8 (over z, y), feat: 4 (over x, core).
Axes of the slice: x: 2, y: 2, z: 4, core: 2. Of those that a mesh axis runs over, the one named last changes fastest.
Arguments:
- grad_pre2: bfloat16 [16384, 512], P('dom', 'feat'), may hold values from -6 to 6
- aggregated2: bfloat16 [16384, 512], P('dom', 'feat'), may hold values from -6 to 6
- weight2: bfloat16 [512, 512], P('feat'), may hold values from -0.25 to 0.25
- pre1: bfloat16 [16384, 512], P('dom', 'feat'), may hold values from -6 to 6
- aggregated1: bfloat16 [16384, 512], P('dom', 'feat'), may hold values from -6 to 6
- weight1: bfloat16 [512, 512], P('feat'), may hold values from -0.25 to 0.25
- blocks: bfloat16 [128, 6, 128, 128], P('dom'), may hold values from -0.21875 to 0.21875
- targets: int32 [128, 6], P('dom'), may hold values from 0 to 127, as said below
Outputs:
- grad_weight2: float32 [512, 512], P('feat')
- grad_weight1: float32 [512, 512], P('feat')
- grad_input: bfloat16 [16384, 512], P('dom', 'feat')
The draws below stay inside these ranges and needn't reach their ends.
Inputs may be any that keep to these rules, and one draw needn't show every extreme that they name: `targets`: partition p holds row tiles p * 16 to p * 16 + 15. Entry 0 of a row tile's list is the tile itself. Every other entry names a tile of partition p + o with -2 <= o <= 2: one of that partition's last 8 tiles if o < 0, one of its first 8 tiles if o > 0, any of its tiles if o = 0. The first row tile of every partition names partitions p - 2, p - 1, p + 1 and p + 2 wherever they exist; the number of blocks that name another partition varies from tile to tile.
All inputs are finite; a program needn't handle non-finite values.
Results may differ from the reference program's by a relative error of at most 0.015.
Values may be sent and summed in bfloat16 or wider, within the bound.
No kernel may reach another device: no remote copies, remote signals or barrier semaphores. Data moves between devices by JAX's collectives and lax.ppermute only.
A program may use at most 64 MiB of HBM per device.

```python
import math
import jax
import jax.numpy as jnp
from jax import lax

D = 512
TILE = 128
BLOCKS = 6
REACH = 2
TD = 16
BT = 8
NTILES = 128
NODES = 16384


def draw_targets(key, part):
    tile_index = jnp.arange(NTILES, dtype=jnp.int32)
    device = tile_index // TD
    local_idx = tile_index % TD
    domains = NTILES // TD
    extra = BLOCKS - 1
    key_offset = jax.random.fold_in(key, 11)
    key_bound = jax.random.fold_in(key, 23)
    key_any = jax.random.fold_in(key, 37)
    offset = jax.random.randint(key_offset, (NTILES, extra), -REACH, REACH + 1)
    forced_list = jnp.concatenate([-jnp.arange(REACH, 0, -1, dtype=jnp.int32), jnp.arange(1, REACH + 1, dtype=jnp.int32), jnp.zeros((extra - 2 * REACH,), jnp.int32)])
    column = jnp.arange(extra, dtype=jnp.int32)
    use_forced = (local_idx[:, None] == 0) & (column[None, :] < 2 * REACH)
    offset = jnp.where(use_forced, forced_list[None, :], offset)
    other_dev = device[:, None] + offset
    in_range = (other_dev >= 0) & (other_dev < domains)
    offset = jnp.where(in_range, offset, 0)
    edge_pick = jax.random.randint(key_bound, (NTILES, extra), 0, BT)
    any_pick = jax.random.randint(key_any, (NTILES, extra), 0, TD)
    within = jnp.where(offset < 0, TD - 1 - edge_pick, jnp.where(offset > 0, edge_pick, any_pick))
    chosen = (device[:, None] + offset) * TD + within
    return jnp.concatenate([tile_index[:, None], chosen], axis=1).astype(jnp.int32)


def block_levels(stream_key, dims, cuts, least, high):
    def one(dim, shards_of):
        draws = jax.random.uniform(jax.random.fold_in(jax.random.fold_in(stream_key, 6), dim), (shards_of,), jnp.float32, least / len(cuts), high / len(cuts))
        return jnp.repeat(jnp.exp(draws), dims[dim] // shards_of).reshape((-1,) + (1,) * (len(dims) - dim - 1))

    level = one(*cuts[0])
    for cut in cuts[1:]:
        level = level * one(*cut)
    return level


def gaussian(own_key, shape, spread, bound, split=(), kind=jnp.bfloat16):
    array = jax.random.normal(own_key, shape, jnp.float32) * spread
    if len(split) > 0:
        array = block_levels(own_key, shape, split, -0.22, 0.18) * array
    return jnp.clip(array, min=-bound, max=bound).astype(kind)


def setup_inputs(seed: int = 0) -> dict:
    seeds = jax.random.split(jax.random.key(seed), 9)
    grad_pre2 = gaussian(seeds[0], (NODES, D), 1.0, 6.0, ((0, 8), (1, 4)))
    aggregated2 = gaussian(seeds[1], (NODES, D), 1.0, 6.0, ((0, 8), (1, 4)))
    weight2 = gaussian(seeds[2], (D, D), D ** -0.5, 0.25, ((0, 4),))
    pre1 = gaussian(seeds[3], (NODES, D), 1.0, 6.0, ((0, 8), (1, 4)))
    aggregated1 = gaussian(seeds[4], (NODES, D), 1.0, 6.0, ((0, 8), (1, 4)))
    weight1 = gaussian(seeds[5], (D, D), D ** -0.5, 0.25, ((0, 4),))
    blocks = gaussian(seeds[6], (NTILES, BLOCKS, TILE, TILE), (BLOCKS * TILE) ** -0.5, 0.21875, ((0, 8),))
    targets = draw_targets(jax.random.fold_in(seeds[8], 71), 0)
    return dict(grad_pre2=grad_pre2, aggregated2=aggregated2, weight2=weight2, pre1=pre1, aggregated1=aggregated1, weight1=weight1, blocks=blocks, targets=targets)


def spread_tiles(blocks, targets, values):
    tile_total = targets.shape[0]
    tile_size = blocks.shape[2]
    col_count = values.shape[1]
    groups = tile_total // TD
    window = (2 * REACH + 1) * TD
    source_groups = values.reshape(groups, TD, tile_size, col_count)
    block_groups = blocks.reshape(groups, TD, BLOCKS, tile_size, tile_size)
    target_groups = targets.reshape(groups, TD * BLOCKS).astype(jnp.int32)
    group_ids = jnp.arange(groups, dtype=jnp.int32)
    own_mask = jnp.arange(window, dtype=jnp.int32) // TD == REACH

    def accumulate(totals, group_item):
        block_group, target_group, source_group, group_id = group_item
        products = jnp.einsum('rkij,rjc->rkic', block_group.astype(jnp.float32), source_group.astype(jnp.float32))
        base = (group_id - REACH) * TD
        relative = (target_group - base + 0 * REACH).astype(jnp.int32)
        local = jax.ops.segment_sum(products.reshape(TD * BLOCKS, tile_size, col_count), relative, num_segments=window)
        rounded = lax.optimization_barrier(local.astype(jnp.bfloat16)).astype(jnp.float32)
        local = jnp.where(own_mask[:, None, None], local, rounded)
        start = (group_id * TD).astype(jnp.int32)
        zero = jnp.zeros((), jnp.int32)
        current = lax.dynamic_slice(totals, (start, zero, zero), (window, tile_size, col_count))
        totals = lax.dynamic_update_slice(totals, current + local, (start, zero, zero))
        return (totals, None)
    start_total = jnp.zeros((tile_total + 2 * REACH * TD, tile_size, col_count), jnp.float32)
    totals, unused = lax.scan(accumulate, start_total, (block_groups, target_groups, source_groups, group_ids))
    totals = totals[REACH * TD:REACH * TD + tile_total]
    return totals.reshape(tile_total * tile_size, col_count)

def reference(grad_pre2, aggregated2, weight2, pre1, aggregated1, weight1, blocks, targets):
    grad_scale = 1.0 / math.sqrt(NODES)
    grad_weight2 = jnp.dot(aggregated2.T, grad_pre2, preferred_element_type=jnp.float32) * grad_scale
    grad_agg2 = jnp.dot(grad_pre2, weight2.T, preferred_element_type=jnp.float32).astype(jnp.bfloat16)
    grad_hidden1 = spread_tiles(blocks, targets, grad_agg2)
    grad_pre1 = jnp.where(pre1 > 0, grad_hidden1, 0.0).astype(jnp.bfloat16)
    grad_weight1 = jnp.dot(aggregated1.T, grad_pre1, preferred_element_type=jnp.float32) * grad_scale
    grad_agg1 = jnp.dot(grad_pre1, weight1.T, preferred_element_type=jnp.float32).astype(jnp.bfloat16)
    grad_input = spread_tiles(blocks, targets, grad_agg1).astype(jnp.bfloat16)
    return (grad_weight2, grad_weight1, grad_input)
```

```python
import functools
import math

import jax
import jax.numpy as jnp
from jax import lax
from jax.experimental import pallas as pl
from jax.experimental.pallas import tpu as pltpu
from jax.sharding import PartitionSpec as P

REACH = 2
CHUNKS = 2
VMEM = pl.BlockSpec(memory_space=pltpu.VMEM)
ANY = pl.BlockSpec(memory_space=pl.ANY)
SMEM = pl.BlockSpec(memory_space=pltpu.SMEM)


def shifted(value, axis, steps):
    count = lax.axis_size(axis)
    first, last = max(0, -steps), min(count, count - steps)
    return lax.ppermute(value, axis, [(s, s + steps) for s in range(first, last)])


def flipped(value, axis, mask):
    count = lax.axis_size(axis)
    return lax.ppermute(value, axis, [(s, s ^ mask) for s in range(count)])


def gather_pieces(value, axis):
    pieces = {0: value}
    mask = lax.axis_size(axis) // 2
    while mask:
        pieces.update({m | mask: flipped(v, axis, mask) for m, v in list(pieces.items())})
        mask //= 2
    return [pieces[m] for m in sorted(pieces)]


def spread_kernel(tiles, slots_ref, *refs):
    chunks = len(tiles)
    pieces = refs[0].shape[0]
    weight_ref, blocks_hbm = refs[0], refs[1]
    piece_refs = refs[2 : 2 + chunks * pieces]
    own_ref = refs[2 + chunks * pieces]
    out_refs = refs[3 + chunks * pieces : -4]
    values, blocks, total, sems = refs[-4:]
    tile_count, count, size, _ = blocks.shape
    for r in range(tile_count):
        pltpu.make_async_copy(blocks_hbm.at[r], blocks.at[r], sems.at[r]).start()
    total[...] = jnp.zeros_like(total)
    for c, tile_list in enumerate(tiles):
        for i, r in enumerate(tile_list):
            rows = pl.ds(i * size, size)
            value = jnp.zeros((size, size), jnp.float32)
            for m in range(pieces):
                value += lax.dot_general(
                    piece_refs[c * pieces + m][rows, :],
                    weight_ref[m],
                    (((1,), (1,)), ((), ())),
                    preferred_element_type=jnp.float32,
                )
            values[r] = value.astype(values.dtype)

    def body(r, carry):
        pltpu.make_async_copy(blocks_hbm.at[r], blocks.at[r], sems.at[r]).wait()
        products = jnp.dot(
            blocks[r].reshape(count * size, size), values[r], preferred_element_type=jnp.float32
        )
        for k in range(count):
            slot = slots_ref[r, k]
            total[slot] += products[k * size : (k + 1) * size]
        return carry

    lax.fori_loop(0, tile_count, body, 0, unroll=2)
    own_ref[...] = total[:tile_count]
    per = out_refs[0].shape[0]
    for n, out in enumerate(out_refs):
        out[...] = total[tile_count + n * per : tile_count + (n + 1) * per].astype(out.dtype)


def spread(chunk_pieces, weight, blocks, slots, tiles):
    tile_count, count, size, _ = blocks.shape
    half = tile_count // 2
    per = half // CHUNKS
    remote = 2 * REACH * half
    outs = [jax.ShapeDtypeStruct((tile_count, size, size), jnp.float32)]
    outs += [jax.ShapeDtypeStruct((per, size, size), jnp.bfloat16)] * (remote // per)
    flat = [p for pieces in chunk_pieces for p in pieces]
    results = pl.pallas_call(
        functools.partial(spread_kernel, tiles),
        out_shape=outs,
        in_specs=[SMEM, VMEM, ANY] + [VMEM] * len(flat),
        out_specs=[VMEM] * len(outs),
        scratch_shapes=[
            pltpu.VMEM((tile_count, size, size), jnp.bfloat16),
            pltpu.VMEM(blocks.shape, jnp.bfloat16),
            pltpu.VMEM((tile_count + remote, size, size), jnp.float32),
            pltpu.SemaphoreType.DMA((tile_count,)),
        ],
        cost_estimate=pl.CostEstimate(
            flops=2 * tile_count * (count + weight.shape[0]) * size**3,
            bytes_accessed=blocks.size * 2 + tile_count * size * size * 16,
            transcendentals=0,
        ),
        compiler_params=pltpu.CompilerParams(vmem_limit_bytes=24 << 20),
        name="spread",
    )(slots, weight, blocks, *flat)
    own, sends = results[0], results[1:]
    parts = half // per
    steps = [1, 2, -1, -2]
    received = [[None] * parts for _ in steps]
    for c in range(parts):
        for d in (1, 3, 0, 2):
            received[d][c] = shifted(sends[d * parts + c], "dom", steps[d])
    chunks = []
    for c in range(parts):
        low = own[c * per : (c + 1) * per]
        high = own[half + c * per : half + (c + 1) * per]
        for distance in range(REACH):
            low = low + received[distance][c].astype(jnp.float32)
            high = high + received[REACH + distance][c].astype(jnp.float32)
        chunks.append(jnp.concatenate([low, high], axis=0))
    return chunks


def weight_kernel(scale, chunks, agg_ref, *refs):
    pieces = len(refs) // chunks
    out_ref = refs[-1]
    for m in range(pieces):
        total = None
        row = 0
        for c in range(chunks):
            piece = refs[c * pieces + m]
            rows = piece.shape[0]
            term = lax.dot_general(
                agg_ref[row : row + rows, :],
                piece[...],
                (((0,), (0,)), ((), ())),
                preferred_element_type=jnp.float32,
            )
            total = term if total is None else total + term
            row += rows
        out_ref[m] = (total * scale).astype(out_ref.dtype)


def weight_term(agg, chunk_pieces, scale):
    flat = [p for pieces in chunk_pieces for p in pieces]
    pieces = len(chunk_pieces[0])
    width = agg.shape[1]
    return pl.pallas_call(
        functools.partial(weight_kernel, scale, len(chunk_pieces)),
        out_shape=jax.ShapeDtypeStruct((pieces, width, width), jnp.bfloat16),
        in_specs=[VMEM] * (1 + len(flat)),
        out_specs=VMEM,
        cost_estimate=pl.CostEstimate(
            flops=2 * pieces * agg.shape[0] * width**2,
            bytes_accessed=agg.size * 2 * (1 + pieces),
            transcendentals=0,
        ),
        compiler_params=pltpu.CompilerParams(vmem_limit_bytes=12 << 20),
        name="weight_term",
    )(agg, *flat)


def dom_sum(value):
    count = lax.axis_size("dom")
    mask = 1
    while mask < count:
        other = flipped(value, "dom", mask)
        total = value.astype(jnp.float32) + other.astype(jnp.float32)
        mask *= 2
        value = total.astype(jnp.bfloat16) if mask < count else total
    return value


def unpermute(value):
    pieces, width, _ = value.shape
    index = lax.axis_index("feat")
    order = jnp.arange(pieces) ^ index
    return jnp.take(value, order, axis=0).transpose(1, 0, 2).reshape(width, pieces * width)


def permuted_weight(weight):
    width = weight.shape[0]
    pieces = weight.shape[1] // width
    index = lax.axis_index("feat")
    blocks = weight.reshape(width, pieces, width).transpose(1, 0, 2)
    return jnp.take(blocks, jnp.arange(pieces) ^ index, axis=0)


def shards(grad_pre2, aggregated2, weight2, pre1, aggregated1, weight1, blocks, targets):
    tile_count, _, size, _ = blocks.shape
    half = tile_count // 2
    per = half // CHUNKS
    scale = 1.0 / math.sqrt(grad_pre2.shape[0] * lax.axis_size("dom"))
    width = grad_pre2.shape[1]
    place = lax.axis_index("dom")
    part = targets // tile_count
    offset = part - place
    within = targets - part * tile_count
    slots = jnp.where(
        offset == 0,
        within,
        jnp.where(
            offset > 0,
            tile_count + (offset - 1) * half + within,
            tile_count + REACH * half + (-offset - 1) * half + within - half,
        ),
    ).astype(jnp.int32)
    tiles = [
        [base + c * per + i for base in (0, half) for i in range(per)] for c in range(CHUNKS)
    ]

    def chunked(array):
        tiled = array.reshape(tile_count, size, width)
        return [
            jnp.concatenate(
                [tiled[c * per : (c + 1) * per], tiled[half + c * per : half + (c + 1) * per]],
                axis=0,
            ).reshape(-1, width)
            for c in range(CHUNKS)
        ]

    w2, w1 = permuted_weight(weight2), permuted_weight(weight1)
    gathered2 = [gather_pieces(c, "feat") for c in chunked(grad_pre2)]
    hidden = spread(gathered2, w2, blocks, slots, tiles)
    second = weight_term(jnp.concatenate(chunked(aggregated2), axis=0), gathered2, scale)
    grad_pre1 = [
        jnp.where(p > 0, h.reshape(-1, width), 0.0).astype(jnp.bfloat16)
        for p, h in zip(chunked(pre1), hidden)
    ]
    gathered1 = [gather_pieces(c, "feat") for c in grad_pre1]
    inputs = spread(gathered1, w1, blocks, slots, tiles)
    first = weight_term(jnp.concatenate(chunked(aggregated1), axis=0), gathered1, scale)
    stacked = [c.astype(jnp.bfloat16).reshape(2, per, size, width) for c in inputs]
    grad_input = jnp.concatenate(stacked, axis=1).reshape(-1, width)
    return (unpermute(dom_sum(second)), unpermute(dom_sum(first)), grad_input)


def solution(mesh):
    in_specs = (
        P("dom", "feat"),
        P("dom", "feat"),
        P("feat", None),
        P("dom", "feat"),
        P("dom", "feat"),
        P("feat", None),
        P("dom", None, None, None),
        P("dom", None),
    )
    out_specs = (P("feat", None), P("feat", None), P("dom", "feat"))
    return jax.shard_map(shards, mesh=mesh, in_specs=in_specs, out_specs=out_specs, check_vma=False)
```

```python
import functools
import math

import jax
import jax.numpy as jnp
from jax import lax
from jax.experimental import pallas as pl
from jax.experimental.pallas import tpu as pltpu
from jax.sharding import PartitionSpec as P


REACH = 2
VMEM = pl.BlockSpec(memory_space=pltpu.VMEM)
ANY = pl.BlockSpec(memory_space=pl.ANY)
SMEM = pl.BlockSpec(memory_space=pltpu.SMEM)


def exchanged(value, axis, partner):
    count = lax.axis_size(axis)
    pairs = [(s, partner(s)) for s in range(count) if 0 <= partner(s) < count]
    return lax.ppermute(value, axis, pairs)


SWAPS = [
    lambda s: ((s + 1) ^ 1) - 1,
    lambda s: s ^ 1,
    lambda s: ((s + 2) ^ 2) - 2,
    lambda s: s ^ 2,
]


def after(value, *earlier):
    return lax.optimization_barrier((value, *earlier))[0]


def gather_pieces(chunks, axis, earlier=()):
    held = [{0: chunk} for chunk in chunks]
    mask = lax.axis_size(axis) // 2
    first = True
    while mask:
        moves = [list(pieces) for pieces in held]
        for step in range(len(moves[0])):
            for c, (pieces, move) in enumerate(zip(held, moves)):
                m = move[step]
                got = exchanged(pieces[m], axis, lambda s, mask=mask: s ^ mask)
                pieces[m | mask] = after(got, *earlier) if first and earlier and c == 0 else got
        first = False
        mask //= 2
    return [[pieces[m] for m in sorted(pieces)] for pieces in held]


def prepare_kernel(targets_hbm, blocks_hbm, *refs):
    count = (len(refs) - 5) // 2
    weight_refs, slots_ref, blocks_ref = refs[:count], refs[count], refs[count + 1]
    outs, (targets_ref, target_sem, block_sem) = refs[count + 2 : -3], refs[-3:]
    block_copy = pltpu.make_async_copy(blocks_hbm, blocks_ref, block_sem)
    target_copy = pltpu.make_async_copy(targets_hbm, targets_ref, target_sem)
    block_copy.start()
    target_copy.start()
    place = lax.axis_index("feat")
    for weight_ref, out in zip(weight_refs, outs):
        width, total = weight_ref.shape
        for m in range(total // width):
            start = pl.multiple_of((place ^ m) * width, width)
            out[m * width : (m + 1) * width, :] = weight_ref[:, pl.ds(start, width)].T
    tile_count, entries = slots_ref.shape
    half = tile_count // 2
    index = lax.axis_index("dom")
    odd, upper = index & 1, (index & 2) // 2
    target_copy.wait()

    def body(r, carry):
        for k in range(entries):
            target = targets_ref[r, k]
            part = lax.div(target, jnp.int32(tile_count))
            offset = part - index
            within = target - part * tile_count
            up = offset > 0
            near = jnp.where(up, 1 - odd, odd)
            far = 2 + jnp.where(up, 1 - upper, upper)
            swap = jnp.where(jnp.abs(offset) == 1, near, far)
            outer = tile_count + swap * half + jnp.where(up, within, within - half)
            slots_ref[r, k] = jnp.where(offset == 0, within, outer)
        return carry

    lax.fori_loop(0, tile_count, body, 0)
    block_copy.wait()


def prepare(targets, blocks, weights):
    outs = [
        jax.ShapeDtypeStruct(targets.shape, jnp.int32),
        jax.ShapeDtypeStruct(blocks.shape, blocks.dtype),
    ]
    outs += [jax.ShapeDtypeStruct(w.shape[::-1], w.dtype) for w in weights]
    return pl.pallas_call(
        prepare_kernel,
        out_shape=outs,
        in_specs=[ANY, pl.BlockSpec(memory_space=pltpu.HBM)] + [VMEM] * len(weights),
        out_specs=[SMEM] + [VMEM] * (len(outs) - 1),
        scratch_shapes=[
            pltpu.SMEM(targets.shape, jnp.int32),
            pltpu.SemaphoreType.DMA,
            pltpu.SemaphoreType.DMA,
        ],
        compiler_params=pltpu.CompilerParams(vmem_limit_bytes=8 << 20),
        cost_estimate=pl.CostEstimate(flops=0, bytes_accessed=4 * blocks.size, transcendentals=0),
        name="prepare",
    )(targets, blocks, *weights)


def spread_kernel(chunks, slots_ref, weights, blocks, *refs):
    width = weights.shape[1]
    pieces = weights.shape[0] // width
    piece_refs, (own_ref, *sends, values, total) = (
        refs[: chunks * pieces],
        refs[chunks * pieces :],
    )
    tile_count, count, size, _ = blocks.shape
    total[...] = jnp.zeros_like(total)
    group = 2
    per = tile_count // chunks // group

    def value_body(i, carry, c):
        rows = pl.ds(pl.multiple_of(i * group * size, group * size), group * size)
        left = jnp.concatenate(
            [piece_refs[c * pieces + m][rows, :] for m in range(pieces)], axis=1
        )
        value = jnp.dot(left, weights[...], preferred_element_type=jnp.float32)
        tiles = pl.ds(c * per * group + i * group, group)
        values[tiles] = value.astype(values.dtype).reshape(group, size, width)
        return carry

    for c in range(chunks):
        lax.fori_loop(0, per, functools.partial(value_body, c=c), 0, unroll=2)

    def body(r, carry):
        value = values[r]
        for k in range(count):
            slot = slots_ref[r, k]
            total[slot] += jnp.dot(blocks[r, k], value, preferred_element_type=jnp.float32)
        return carry

    lax.fori_loop(0, tile_count, body, 0, unroll=4)
    own_ref[...] = total[:tile_count]
    half = sends[0].shape[0]
    for n, send in enumerate(sends):
        start = tile_count + n * half
        send[...] = total[start : start + half].astype(send.dtype)


def spread(chunk_pieces, weight, blocks, slots):
    tile_count, count, size, _ = blocks.shape
    half = tile_count // 2
    width = weight.shape[1]
    outs = [jax.ShapeDtypeStruct((tile_count, size, width), jnp.float32)]
    outs += [jax.ShapeDtypeStruct((half, size, width), jnp.bfloat16)] * len(SWAPS)
    flat = [p for pieces in chunk_pieces for p in pieces]
    return pl.pallas_call(
        functools.partial(spread_kernel, len(chunk_pieces)),
        out_shape=outs,
        in_specs=[SMEM] + [VMEM] * (2 + len(flat)),
        out_specs=[VMEM] * len(outs),
        scratch_shapes=[
            pltpu.VMEM((tile_count, size, width), jnp.bfloat16),
            pltpu.VMEM((tile_count + 2 * REACH * half, size, width), jnp.float32),
        ],
        cost_estimate=pl.CostEstimate(
            flops=2 * tile_count * size * width * (count * size + weight.shape[0]),
            bytes_accessed=blocks.size * 2 + tile_count * size * width * 16,
            transcendentals=0,
        ),
        compiler_params=pltpu.CompilerParams(vmem_limit_bytes=16 << 20),
        name="spread",
    )(slots, weight, blocks, *flat)


def join_kernel(masked, own, next_over, across, next_apart, apart, *refs):
    tile_count, size, _ = own.shape
    half = tile_count // 2
    index = lax.axis_index("dom")
    odd, upper = (index & 1) == 1, (index & 2) == 2
    if masked:
        mask, *outs = refs
    else:
        value, other, summed, out = refs
        outs = [out.at[: half * size, :], out.at[half * size :, :]]
        summed[...] = value[...].astype(jnp.float32) + other[...].astype(jnp.float32)

    def write(side, near, far):
        out = outs[side]
        for t in range(half):
            total = own[side * half + t]
            total += near[t].astype(jnp.float32) + far[t].astype(jnp.float32)
            if masked:
                first = (side * half + t) * size
                total = jnp.where(mask[first : first + size, :] > 0, total, 0.0)
            out[t * size : (t + 1) * size, :] = total.astype(out.dtype)

    for is_odd in (False, True):
        for is_upper in (False, True):

            @pl.when((odd == is_odd) & (upper == is_upper))
            def _(is_odd=is_odd, is_upper=is_upper):
                near = [across, next_over] if is_odd else [next_over, across]
                far = [apart, next_apart] if is_upper else [next_apart, apart]
                write(0, near[0], far[0])
                write(1, near[1], far[1])


def boundary(own, sends):
    got = [exchanged(send, "dom", swap) for send, swap in zip(sends, SWAPS)]
    return own, *got


def join(sums, outs, mask=None, terms=()):
    masked = mask is not None
    args = [*sums, mask] if masked else [*sums, *terms]
    return pl.pallas_call(
        functools.partial(join_kernel, masked),
        out_shape=outs,
        in_specs=[VMEM] * len(args),
        out_specs=[VMEM] * len(outs),
        compiler_params=pltpu.CompilerParams(vmem_limit_bytes=8 << 20),
        cost_estimate=pl.CostEstimate(
            flops=0, bytes_accessed=12 * sums[0].size, transcendentals=0
        ),
        name="join",
    )(*args)


def weight_kernel(scale, chunks, agg_ref, *refs):
    pieces = len(refs) // chunks
    out_ref = refs[-1]
    width = agg_ref.shape[1]
    place = lax.axis_index("feat")
    for m in range(pieces):
        total = jnp.zeros((width, width), jnp.float32)
        row = 0
        for c in range(chunks):
            piece = refs[c * pieces + m]
            rows = piece.shape[0]
            total += lax.dot_general(
                agg_ref[row : row + rows, :],
                piece[...],
                (((0,), (0,)), ((), ())),
                preferred_element_type=jnp.float32,
            )
            row += rows
        start = pl.multiple_of((place ^ m) * width, width)
        out_ref[:, pl.ds(start, width)] = (total * scale).astype(out_ref.dtype)


def weight_term(agg, chunk_pieces, scale):
    flat = [p for pieces in chunk_pieces for p in pieces]
    pieces = len(chunk_pieces[0])
    width = agg.shape[1]
    return pl.pallas_call(
        functools.partial(weight_kernel, scale, len(chunk_pieces)),
        out_shape=jax.ShapeDtypeStruct((width, pieces * width), jnp.bfloat16),
        in_specs=[VMEM] * (1 + len(flat)),
        out_specs=VMEM,
        cost_estimate=pl.CostEstimate(
            flops=2 * pieces * agg.shape[0] * width**2,
            bytes_accessed=agg.size * 2 * (1 + pieces),
            transcendentals=0,
        ),
        compiler_params=pltpu.CompilerParams(vmem_limit_bytes=8 << 20),
        name="weight_term",
    )(agg, *flat)


def sum_steps(value, waits=()):
    masks = [1]
    mask = lax.axis_size("dom") // 2
    while mask > 1:
        masks.append(mask)
        mask //= 2
    waits = list(waits)
    for n, mask in enumerate(masks):
        other = exchanged(value, "dom", lambda s, mask=mask: s ^ mask)
        if waits:
            other = after(other, *waits.pop(0))
        if n + 1 == len(masks):
            return value, other
        total = value.astype(jnp.float32) + other.astype(jnp.float32)
        value = total.astype(jnp.bfloat16)


def shards(grad_pre2, aggregated2, weight2, pre1, aggregated1, weight1, blocks, targets):
    nodes, width = grad_pre2.shape
    scale = 1.0 / math.sqrt(nodes * lax.axis_size("dom"))
    rows = nodes // 2
    half = jax.ShapeDtypeStruct((rows, width), jnp.bfloat16)
    slots, blocks, weight2, weight1 = prepare(targets, blocks, [weight2, weight1])
    gathered2 = gather_pieces(
        [grad_pre2[:rows], lax.optimization_barrier(grad_pre2)[rows:]], "feat", [weight2]
    )
    own, *sends = spread(gathered2, weight2, blocks, slots)
    second = weight_term(after(aggregated2, sends[0]), gathered2, scale)
    sums = boundary(own, sends)
    sums = [*sums[:2], *lax.optimization_barrier((second, *sums[2:]))[1:]]
    grad_pre1 = join(sums, [half, half], mask=pre1)
    gathered1 = gather_pieces(grad_pre1, "feat")
    first = weight_term(aggregated1, gathered1, scale)
    own, *sends = spread(gathered1, weight1, blocks, slots)
    second = sum_steps(after(second, grad_pre1[0]), [[gathered1[0][2]], [sends[0]]])
    second = second[0].astype(jnp.float32) + second[1].astype(jnp.float32)
    sums = boundary(own, sends)
    outs = [
        jax.ShapeDtypeStruct(first.shape, jnp.float32),
        jax.ShapeDtypeStruct((nodes, width), jnp.bfloat16),
    ]
    first, grad_input = join(sums, outs, terms=sum_steps(first))
    return (second, first, grad_input)


def solution(mesh):
    in_specs = (
        P("dom", "feat"),
        P("dom", "feat"),
        P("feat", None),
        P("dom", "feat"),
        P("dom", "feat"),
        P("feat", None),
        P("dom", None, None, None),
        P("dom", None),
    )
    out_specs = (P("feat", None), P("feat", None), P("dom", "feat"))
    return jax.shard_map(shards, mesh=mesh, in_specs=in_specs, out_specs=out_specs, check_vma=False)
```

```python
import functools
import math

import jax
import jax.numpy as jnp
from jax import lax
from jax.experimental import pallas as pl
from jax.experimental.pallas import tpu as pltpu
from jax.sharding import PartitionSpec as P


VMEM = pl.BlockSpec(memory_space=pltpu.VMEM)
ANY = pl.BlockSpec(memory_space=pl.ANY)
SMEM = pl.BlockSpec(memory_space=pltpu.SMEM)


def exchanged(value, axis, partner):
    count = lax.axis_size(axis)
    pairs = [(s, partner(s)) for s in range(count) if 0 <= partner(s) < count]
    return lax.ppermute(value, axis, pairs)


SWAPS = [
    lambda s: ((s + 1) ^ 1) - 1,
    lambda s: s ^ 1,
    lambda s: ((s + 2) ^ 2) - 2,
    lambda s: s ^ 2,
]


def after(value, *earlier):
    return lax.optimization_barrier((value, *earlier))[0]


def gather_pieces(chunks, axis, earlier=()):
    held = [{0: chunk} for chunk in chunks]
    mask = lax.axis_size(axis) // 2
    first = True
    while mask:
        moves = [list(pieces) for pieces in held]
        for step in range(len(moves[0])):
            for c, (pieces, move) in enumerate(zip(held, moves)):
                m = move[step]
                got = exchanged(pieces[m], axis, lambda s, mask=mask: s ^ mask)
                pieces[m | mask] = after(got, *earlier) if first and earlier and c == 0 else got
        first = False
        mask //= 2
    return [[pieces[m] for m in sorted(pieces)] for pieces in held]


def prepare_kernel(targets_hbm, blocks_hbm, *refs):
    count = (len(refs) - 5) // 2
    weight_refs, slots_ref, blocks_ref = refs[:count], refs[count], refs[count + 1]
    outs, (targets_ref, target_sem, block_sem) = refs[count + 2 : -3], refs[-3:]
    block_copy = pltpu.make_async_copy(blocks_hbm, blocks_ref, block_sem)
    target_copy = pltpu.make_async_copy(targets_hbm, targets_ref, target_sem)
    block_copy.start()
    target_copy.start()
    place = lax.axis_index("feat")
    for weight_ref, out in zip(weight_refs, outs):
        width, total = weight_ref.shape
        for m in range(total // width):
            start = pl.multiple_of((place ^ m) * width, width)
            out[m * width : (m + 1) * width, :] = weight_ref[:, pl.ds(start, width)].T
    tile_count, entries = slots_ref.shape
    half = tile_count // 2
    index = lax.axis_index("dom")
    odd, upper = index & 1, (index & 2) // 2
    target_copy.wait()

    def body(r, carry):
        for k in range(entries):
            target = targets_ref[r, k]
            part = lax.div(target, jnp.int32(tile_count))
            offset = part - index
            within = target - part * tile_count
            up = offset > 0
            near = jnp.where(up, 1 - odd, odd)
            far = 2 + jnp.where(up, 1 - upper, upper)
            swap = jnp.where(jnp.abs(offset) == 1, near, far)
            outer = tile_count + swap * half + jnp.where(up, within, within - half)
            slots_ref[r, k] = jnp.where(offset == 0, within, outer)
        return carry

    lax.fori_loop(0, tile_count, body, 0)
    block_copy.wait()


def prepare(targets, blocks, weights):
    outs = [
        jax.ShapeDtypeStruct(targets.shape, jnp.int32),
        jax.ShapeDtypeStruct(blocks.shape, blocks.dtype),
    ]
    outs += [jax.ShapeDtypeStruct(w.shape[::-1], w.dtype) for w in weights]
    return pl.pallas_call(
        prepare_kernel,
        out_shape=outs,
        in_specs=[ANY, pl.BlockSpec(memory_space=pltpu.HBM)] + [VMEM] * len(weights),
        out_specs=[SMEM] + [VMEM] * (len(outs) - 1),
        scratch_shapes=[
            pltpu.SMEM(targets.shape, jnp.int32),
            pltpu.SemaphoreType.DMA,
            pltpu.SemaphoreType.DMA,
        ],
        compiler_params=pltpu.CompilerParams(vmem_limit_bytes=8 << 20),
        cost_estimate=pl.CostEstimate(flops=0, bytes_accessed=4 * blocks.size, transcendentals=0),
        name="prepare",
    )(targets, blocks, *weights)


def unrolling(count):
    return max(n for n in range(1, 7) if count % n == 0)


def spread_kernel(first, tiles, slots_ref, weights, blocks, *refs):
    last = tiles[1] == blocks.shape[0]
    width = weights.shape[1]
    pieces = weights.shape[0] // width
    piece_refs, refs = refs[:pieces], refs[pieces:]
    total, sends, values = refs[0 if first else 1], refs[1 if first else 2 : -1], refs[-1]
    tile_count, count, size, _ = blocks.shape
    if first:
        total[...] = jnp.zeros_like(total)
    group = 2
    for i in range((tiles[1] - tiles[0]) // group):
        rows = slice(i * group * size, (i + 1) * group * size)
        left = jnp.concatenate([piece[rows, :] for piece in piece_refs], axis=1)
        value = jnp.dot(left, weights[...], preferred_element_type=jnp.float32)
        value = value.astype(values.dtype).reshape(group, size, width)
        values[i * group : (i + 1) * group] = value

    def body(i, carry):
        value = values[i]
        r = tiles[0] + i
        for k in range(count):
            slot = slots_ref[r, k]
            total[slot] += jnp.dot(blocks[r, k], value, preferred_element_type=jnp.float32)
        return carry

    lax.fori_loop(0, tiles[1] - tiles[0], body, 0, unroll=unrolling(tiles[1] - tiles[0]))
    half = tile_count // 2
    for n, send in enumerate(sends if last else ()):
        start = tile_count + n * half
        send[...] = total[start : start + half].astype(send.dtype)


def spread(tiles, pieces, weight, blocks, slots, total=None):
    tile_count, count, size, _ = blocks.shape
    half = tile_count // 2
    width = weight.shape[1]
    held = tiles[1] - tiles[0]
    outs = [
        jax.ShapeDtypeStruct((tile_count + len(SWAPS) * half, size, width), jnp.float32)
    ]
    if tiles[1] == tile_count:
        outs += [jax.ShapeDtypeStruct((half, size, width), jnp.bfloat16)] * len(SWAPS)
    args = [slots, weight, blocks, *pieces]
    aliases = {}
    if total is not None:
        aliases[len(args)] = 0
        args.append(total)
    return pl.pallas_call(
        functools.partial(spread_kernel, total is None, tiles),
        out_shape=outs,
        in_specs=[SMEM] + [VMEM] * (len(args) - 1),
        out_specs=[VMEM] * len(outs),
        input_output_aliases=aliases,
        scratch_shapes=[pltpu.VMEM((held, size, width), jnp.bfloat16)],
        cost_estimate=pl.CostEstimate(
            flops=2 * held * size * width * (count * size + weight.shape[0]),
            bytes_accessed=held * size * width * 2 * (count + 8),
            transcendentals=0,
        ),
        compiler_params=pltpu.CompilerParams(vmem_limit_bytes=16 << 20),
        name="spread",
    )(*args)


def join_kernel(masked, tile_count, own, next_over, across, next_apart, apart, *refs):
    size = own.shape[1]
    half = tile_count // 2
    index = lax.axis_index("dom")
    odd, upper = (index & 1) == 1, (index & 2) == 2
    if masked:
        mask, *outs = refs
    else:
        outs = refs
    places = [(out, i) for out in outs for i in range(out.shape[0] // size)]

    def write(tile, near, far):
        total = own[tile]
        total += near[tile % half].astype(jnp.float32) + far[tile % half].astype(jnp.float32)
        if masked:
            total = jnp.where(mask[tile * size : (tile + 1) * size, :] > 0, total, 0.0)
        out, i = places[tile]
        out[i * size : (i + 1) * size, :] = total.astype(out.dtype)

    for is_odd in (False, True):
        for is_upper in (False, True):

            @pl.when((odd == is_odd) & (upper == is_upper))
            def _(is_odd=is_odd, is_upper=is_upper):
                near = [across, next_over] if is_odd else [next_over, across]
                far = [apart, next_apart] if is_upper else [next_apart, apart]
                for tile in range(tile_count):
                    write(tile, near[tile // half], far[tile // half])


def boundary(own, sends):
    got = [exchanged(send, "dom", swap) for send, swap in zip(sends, SWAPS)]
    return own, *got


def join(sums, outs, mask=None):
    masked = mask is not None
    args = [*sums, mask] if masked else list(sums)
    return pl.pallas_call(
        functools.partial(join_kernel, masked, 2 * sums[1].shape[0]),
        out_shape=outs,
        in_specs=[VMEM] * len(args),
        out_specs=[VMEM] * len(outs),
        compiler_params=pltpu.CompilerParams(vmem_limit_bytes=8 << 20),
        cost_estimate=pl.CostEstimate(
            flops=0, bytes_accessed=12 * sums[1].size, transcendentals=0
        ),
        name="join",
    )(*args)


def term(left, right):
    return lax.dot_general(left, right, (((0,), (0,)), ((), ())), preferred_element_type=jnp.float32)


def second_kernel(scale, cuts, agg, *refs):
    *chunks, out = refs
    count = len(chunks) // len(cuts)
    for m in range(count):
        total = None
        for c, (first, last) in enumerate(cuts):
            part = term(agg[first:last, :], chunks[c * count + m][...])
            total = part if total is None else total + part
        out[m] = (total * scale).astype(out.dtype)


def first_kernel(scale, cuts, seconds, *refs):
    count = seconds.shape[0]
    pieces, chunks, (keep, send) = refs[:count], refs[count:-2], refs[-2:]
    odd = (lax.axis_index("dom") & 1) == 1
    for m in range(count):
        total = None
        for (first, last), chunk in zip(cuts, chunks):
            part = term(pieces[m][first:last, :], chunk[...])
            total = part if total is None else total + part
        total = (total * scale).astype(send.dtype)
        keep[m] = jnp.where(odd, seconds[m], total)
        send[m] = jnp.where(odd, total, seconds[m])


def parted_kernel(kept, got, second_out, *blocks):
    odd = (lax.axis_index("dom") & 1) == 1
    place = lax.axis_index("feat")
    width = kept.shape[1]
    for m, block in enumerate(blocks):
        block[...] = jnp.where(odd, got[m], kept[m])
        columns = pl.ds(pl.multiple_of((place ^ m) * width, width), width)
        second_out[:, columns] = jnp.where(odd, kept[m], got[m]).astype(second_out.dtype)


def placed_kernel(*refs):
    *blocks, out = refs
    place = lax.axis_index("feat")
    width = out.shape[0]
    for m, block in enumerate(blocks):
        columns = pl.ds(pl.multiple_of((place ^ m) * width, width), width)
        out[:, columns] = block[...].astype(out.dtype)


def small_call(kernel, outs, args, flops=0):
    return pl.pallas_call(
        kernel,
        out_shape=outs,
        in_specs=[VMEM] * len(args),
        out_specs=jax.tree.map(lambda _: VMEM, outs),
        cost_estimate=pl.CostEstimate(
            flops=flops, bytes_accessed=sum(2 * a.size for a in args), transcendentals=0
        ),
        compiler_params=pltpu.CompilerParams(vmem_limit_bytes=8 << 20),
    )(*args)


def added(value, other):
    return (value.astype(jnp.float32) + other.astype(jnp.float32)).astype(jnp.bfloat16)


def dom_sums(keep, send):
    value = added(keep, exchanged(send, "dom", lambda s: s ^ 1))
    mask = lax.axis_size("dom") // 2
    while mask > 1:
        other = exchanged(value, "dom", lambda s, mask=mask: s ^ mask)
        value = added(value, other)
        mask //= 2
    return value, exchanged(value, "dom", lambda s: s ^ 1)


def shards(grad_pre2, aggregated2, weight2, pre1, aggregated1, weight1, blocks, targets):
    nodes, width = grad_pre2.shape
    scale = 1.0 / math.sqrt(nodes * lax.axis_size("dom"))
    tile_count, _, size, _ = blocks.shape
    cut = tile_count * 5 // 8
    tiles = [(0, cut), (cut, tile_count)]
    cuts = [(t[0] * size, t[1] * size) for t in tiles]
    parts = [jax.ShapeDtypeStruct((r[1] - r[0], width), jnp.bfloat16) for r in cuts]
    slots, blocks, weight2, weight1 = prepare(targets, blocks, [weight2, weight1])

    chunks = [grad_pre2[: cuts[0][1]], lax.optimization_barrier(grad_pre2)[cuts[0][1] :]]
    gathered = gather_pieces(chunks, "feat", [weight2])
    count = len(gathered[0])
    flops = 2 * nodes * count * width**2
    grads = jax.ShapeDtypeStruct((count, width, width), jnp.bfloat16)
    wide = jax.ShapeDtypeStruct((width, count * width), jnp.float32)
    own, *sends = layer(tiles, gathered, weight2, blocks, slots)
    sums = boundary(own, sends)
    (held,) = gather_pieces([aggregated1], "feat")
    seconds = small_call(
        functools.partial(second_kernel, scale, cuts),
        grads,
        [after(aggregated2, sends[0]), *gathered[0], *gathered[1]],
        flops,
    )
    grad_pre1 = join(sums, parts, mask=pre1)

    gathered = gather_pieces(grad_pre1, "feat")
    keep, send = small_call(
        functools.partial(first_kernel, scale, cuts),
        [grads, grads],
        [seconds, *held, *grad_pre1],
        flops,
    )
    kept, got = dom_sums(keep, send)
    own, *sends = layer(tiles, gathered, weight1, blocks, slots)
    sums = boundary(own, sends)
    block = jax.ShapeDtypeStruct((width, width), jnp.bfloat16)
    second, *firsts = small_call(parted_kernel, [wide, *[block] * count], [kept, got])
    firsts = [firsts[0]] + [
        exchanged(firsts[m], "feat", lambda s, m=m: s ^ m) for m in range(1, count)
    ]
    first = small_call(placed_kernel, wide, firsts)
    (grad_input,) = join(sums, [jax.ShapeDtypeStruct((nodes, width), jnp.bfloat16)])
    return (second, first, grad_input)


def layer(tiles, gathered, weight, blocks, slots):
    total = None
    for part, pieces in zip(tiles, gathered):
        total, *sends = spread(part, pieces, weight, blocks, slots, total)
    return total, *sends


def solution(mesh):
    in_specs = (
        P("dom", "feat"),
        P("dom", "feat"),
        P("feat", None),
        P("dom", "feat"),
        P("dom", "feat"),
        P("feat", None),
        P("dom", None, None, None),
        P("dom", None),
    )
    out_specs = (P("feat", None), P("feat", None), P("dom", "feat"))
    return jax.shard_map(shards, mesh=mesh, in_specs=in_specs, out_specs=out_specs, check_vma=False)
```

```python
import functools
import math

import jax
import jax.numpy as jnp
from jax import lax
from jax.experimental import pallas as pl
from jax.experimental.pallas import tpu as pltpu
from jax.sharding import PartitionSpec as P


VMEM = pl.BlockSpec(memory_space=pltpu.VMEM)
ANY = pl.BlockSpec(memory_space=pl.ANY)
SMEM = pl.BlockSpec(memory_space=pltpu.SMEM)


def exchanged(value, axis, partner):
    count = lax.axis_size(axis)
    pairs = [(s, partner(s)) for s in range(count) if 0 <= partner(s) < count]
    return lax.ppermute(value, axis, pairs)


SWAPS = [
    lambda s: ((s + 1) ^ 1) - 1,
    lambda s: s ^ 1,
    lambda s: ((s + 2) ^ 2) - 2,
    lambda s: s ^ 2,
]


def after(value, *earlier):
    return lax.optimization_barrier((value, *earlier))[0]


def gather_pieces(chunks, axis, earlier=()):
    held = [{0: chunk} for chunk in chunks]
    mask = lax.axis_size(axis) // 2
    first = True
    while mask:
        moves = [list(pieces) for pieces in held]
        for step in range(len(moves[0])):
            for c, (pieces, move) in enumerate(zip(held, moves)):
                m = move[step]
                got = exchanged(pieces[m], axis, lambda s, mask=mask: s ^ mask)
                pieces[m | mask] = after(got, *earlier) if first and earlier and c == 0 else got
        first = False
        mask //= 2
    return [[pieces[m] for m in sorted(pieces)] for pieces in held]


def prepare_kernel(targets_hbm, blocks_hbm, *refs):
    count = (len(refs) - 5) // 2
    weight_refs, slots_ref, blocks_ref = refs[:count], refs[count], refs[count + 1]
    outs, (targets_ref, target_sem, block_sem) = refs[count + 2 : -3], refs[-3:]
    block_copy = pltpu.make_async_copy(blocks_hbm, blocks_ref, block_sem)
    target_copy = pltpu.make_async_copy(targets_hbm, targets_ref, target_sem)
    block_copy.start()
    target_copy.start()
    place = lax.axis_index("feat")
    for weight_ref, out in zip(weight_refs, outs):
        width, total = weight_ref.shape
        for m in range(total // width):
            start = pl.multiple_of((place ^ m) * width, width)
            out[m * width : (m + 1) * width, :] = weight_ref[:, pl.ds(start, width)].T
    tile_count, entries = slots_ref.shape
    half = tile_count // 2
    index = lax.axis_index("dom")
    odd, upper = index & 1, (index & 2) // 2
    target_copy.wait()

    def body(r, carry):
        for k in range(entries):
            target = targets_ref[r, k]
            part = lax.div(target, jnp.int32(tile_count))
            offset = part - index
            within = target - part * tile_count
            up = offset > 0
            near = jnp.where(up, 1 - odd, odd)
            far = 2 + jnp.where(up, 1 - upper, upper)
            swap = jnp.where(jnp.abs(offset) == 1, near, far)
            outer = tile_count + swap * half + jnp.where(up, within, within - half)
            slots_ref[r, k] = jnp.where(offset == 0, within, outer)
        return carry

    lax.fori_loop(0, tile_count, body, 0)
    block_copy.wait()


def prepare(targets, blocks, weights):
    outs = [
        jax.ShapeDtypeStruct(targets.shape, jnp.int32),
        jax.ShapeDtypeStruct(blocks.shape, blocks.dtype),
    ]
    outs += [jax.ShapeDtypeStruct(w.shape[::-1], w.dtype) for w in weights]
    return pl.pallas_call(
        prepare_kernel,
        out_shape=outs,
        in_specs=[ANY, pl.BlockSpec(memory_space=pltpu.HBM)] + [VMEM] * len(weights),
        out_specs=[SMEM] + [VMEM] * (len(outs) - 1),
        scratch_shapes=[
            pltpu.SMEM(targets.shape, jnp.int32),
            pltpu.SemaphoreType.DMA,
            pltpu.SemaphoreType.DMA,
        ],
        compiler_params=pltpu.CompilerParams(vmem_limit_bytes=8 << 20),
        cost_estimate=pl.CostEstimate(flops=0, bytes_accessed=4 * blocks.size, transcendentals=0),
        name="prepare",
    )(targets, blocks, *weights)


def unrolling(count):
    return max(n for n in range(1, 7) if count % n == 0)


def spread_kernel(first, tiles, slots_ref, weights, blocks, *refs):
    last = tiles[1] == blocks.shape[0]
    width = weights.shape[1]
    pieces = weights.shape[0] // width
    piece_refs, refs = refs[:pieces], refs[pieces:]
    total, sends, values = refs[0 if first else 1], refs[1 if first else 2 : -1], refs[-1]
    tile_count, count, size, _ = blocks.shape
    if first:
        total[...] = jnp.zeros_like(total)
    group = 2
    for i in range((tiles[1] - tiles[0]) // group):
        rows = slice(i * group * size, (i + 1) * group * size)
        left = jnp.concatenate([piece[rows, :] for piece in piece_refs], axis=1)
        value = jnp.dot(left, weights[...], preferred_element_type=jnp.float32)
        value = value.astype(values.dtype).reshape(group, size, width)
        values[i * group : (i + 1) * group] = value

    def body(i, carry):
        value = values[i]
        r = tiles[0] + i
        for k in range(count):
            slot = slots_ref[r, k]
            total[slot] += jnp.dot(blocks[r, k], value, preferred_element_type=jnp.float32)
        return carry

    lax.fori_loop(0, tiles[1] - tiles[0], body, 0, unroll=unrolling(tiles[1] - tiles[0]))
    half = tile_count // 2
    for n, send in enumerate(sends if last else ()):
        start = tile_count + n * half
        send[...] = total[start : start + half].astype(send.dtype)


def spread(tiles, pieces, weight, blocks, slots, total=None):
    tile_count, count, size, _ = blocks.shape
    half = tile_count // 2
    width = weight.shape[1]
    held = tiles[1] - tiles[0]
    outs = [
        jax.ShapeDtypeStruct((tile_count + len(SWAPS) * half, size, width), jnp.float32)
    ]
    if tiles[1] == tile_count:
        outs += [jax.ShapeDtypeStruct((half, size, width), jnp.bfloat16)] * len(SWAPS)
    args = [slots, weight, blocks, *pieces]
    aliases = {}
    if total is not None:
        aliases[len(args)] = 0
        args.append(total)
    return pl.pallas_call(
        functools.partial(spread_kernel, total is None, tiles),
        out_shape=outs,
        in_specs=[SMEM] + [VMEM] * (len(args) - 1),
        out_specs=[VMEM] * len(outs),
        input_output_aliases=aliases,
        scratch_shapes=[pltpu.VMEM((held, size, width), jnp.bfloat16)],
        cost_estimate=pl.CostEstimate(
            flops=2 * held * size * width * (count * size + weight.shape[0]),
            bytes_accessed=held * size * width * 2 * (count + 8),
            transcendentals=0,
        ),
        compiler_params=pltpu.CompilerParams(vmem_limit_bytes=16 << 20),
        name="spread",
    )(*args)


def join_kernel(masked, tile_count, own, next_over, across, next_apart, apart, *refs):
    size = own.shape[1]
    half = tile_count // 2
    index = lax.axis_index("dom")
    odd, upper = (index & 1) == 1, (index & 2) == 2
    if masked:
        mask, *outs = refs
    else:
        grad, other, second, first, *outs = refs

        @pl.when(odd)
        def _():
            second[...] = grad[...].astype(second.dtype)
            first[...] = other[...].astype(first.dtype)

        @pl.when(jnp.logical_not(odd))
        def _():
            second[...] = other[...].astype(second.dtype)
            first[...] = grad[...].astype(first.dtype)

    places = [(out, i) for out in outs for i in range(out.shape[0] // size)]

    def write(tile, near, far):
        total = own[tile]
        total += near[tile % half].astype(jnp.float32) + far[tile % half].astype(jnp.float32)
        if masked:
            total = jnp.where(mask[tile * size : (tile + 1) * size, :] > 0, total, 0.0)
        out, i = places[tile]
        out[i * size : (i + 1) * size, :] = total.astype(out.dtype)

    for is_odd in (False, True):
        for is_upper in (False, True):

            @pl.when((odd == is_odd) & (upper == is_upper))
            def _(is_odd=is_odd, is_upper=is_upper):
                near = [across, next_over] if is_odd else [next_over, across]
                far = [apart, next_apart] if is_upper else [next_apart, apart]
                for tile in range(tile_count):
                    write(tile, near[tile // half], far[tile // half])


def boundary(own, sends):
    got = [exchanged(send, "dom", swap) for send, swap in zip(sends, SWAPS)]
    return own, *got


def join(sums, outs, mask=None, extra=()):
    masked = mask is not None
    args = [*sums, mask] if masked else [*sums, *extra]
    return pl.pallas_call(
        functools.partial(join_kernel, masked, 2 * sums[1].shape[0]),
        out_shape=outs,
        in_specs=[VMEM] * len(args),
        out_specs=[VMEM] * len(outs),
        compiler_params=pltpu.CompilerParams(vmem_limit_bytes=8 << 20),
        cost_estimate=pl.CostEstimate(
            flops=0, bytes_accessed=12 * sums[1].size, transcendentals=0
        ),
        name="join",
    )(*args)


def term(left, right):
    return lax.dot_general(left, right, (((0,), (0,)), ((), ())), preferred_element_type=jnp.float32)


def second_kernel(scale, cuts, agg, *refs):
    *chunks, out = refs
    count = len(chunks) // len(cuts)
    for m in range(count):
        total = None
        for c, (first, last) in enumerate(cuts):
            part = term(agg[first:last, :], chunks[c * count + m][...])
            total = part if total is None else total + part
        out[m] = (total * scale).astype(out.dtype)


def first_kernel(scale, cuts, seconds, *refs):
    count = seconds.shape[0]
    pieces, chunks, (keep, send) = refs[:count], refs[count:-2], refs[-2:]
    odd = (lax.axis_index("dom") & 1) == 1
    for m in range(count):
        total = None
        for (first, last), chunk in zip(cuts, chunks):
            part = term(pieces[m][first:last, :], chunk[...])
            total = part if total is None else total + part
        total = (total * scale).astype(send.dtype)
        keep[m] = jnp.where(odd, seconds[m], total)
        send[m] = jnp.where(odd, total, seconds[m])


def parted_kernel(value, other, total, *blocks):
    for m, block in enumerate(blocks):
        sums = value[m].astype(jnp.float32) + other[m].astype(jnp.float32)
        total[m] = sums.astype(total.dtype)
        block[...] = total[m]


def placed_kernel(total, *refs):
    *blocks, out = refs
    odd = (lax.axis_index("dom") & 1) == 1
    place = lax.axis_index("feat")
    width = out.shape[0]
    for m in range(total.shape[0]):
        columns = pl.ds(pl.multiple_of((place ^ m) * width, width), width)
        out[:, columns] = jnp.where(odd, total[m], blocks[m - 1][...] if m else total[m])


def small_call(kernel, outs, args, flops=0):
    return pl.pallas_call(
        kernel,
        out_shape=outs,
        in_specs=[VMEM] * len(args),
        out_specs=jax.tree.map(lambda _: VMEM, outs),
        cost_estimate=pl.CostEstimate(
            flops=flops, bytes_accessed=sum(2 * a.size for a in args), transcendentals=0
        ),
        compiler_params=pltpu.CompilerParams(vmem_limit_bytes=8 << 20),
    )(*args)


def added(value, other):
    return (value.astype(jnp.float32) + other.astype(jnp.float32)).astype(jnp.bfloat16)


def dom_sums(keep, send):
    value, other = keep, exchanged(send, "dom", lambda s: s ^ 1)
    mask = lax.axis_size("dom") // 2
    while mask > 1:
        value = added(value, other)
        other = exchanged(value, "dom", lambda s, mask=mask: s ^ mask)
        mask //= 2
    return value, other


def shards(grad_pre2, aggregated2, weight2, pre1, aggregated1, weight1, blocks, targets):
    nodes, width = grad_pre2.shape
    scale = 1.0 / math.sqrt(nodes * lax.axis_size("dom"))
    tile_count, _, size, _ = blocks.shape
    cut = tile_count * 5 // 8
    tiles = [(0, cut), (cut, tile_count)]
    cuts = [(t[0] * size, t[1] * size) for t in tiles]
    parts = [jax.ShapeDtypeStruct((r[1] - r[0], width), jnp.bfloat16) for r in cuts]
    slots, blocks, weight2, weight1 = prepare(targets, blocks, [weight2, weight1])

    chunks = [grad_pre2[: cuts[0][1]], lax.optimization_barrier(grad_pre2)[cuts[0][1] :]]
    gathered = gather_pieces(chunks, "feat", [weight2])
    count = len(gathered[0])
    flops = 2 * nodes * count * width**2
    grads = jax.ShapeDtypeStruct((count, width, width), jnp.bfloat16)
    own, *sends = layer(tiles, gathered, weight2, blocks, slots)
    sums = boundary(own, sends)
    (held,) = gather_pieces([aggregated1], "feat")
    seconds = small_call(
        functools.partial(second_kernel, scale, cuts),
        grads,
        [after(aggregated2, sends[0]), *gathered[0], *gathered[1]],
        flops,
    )
    grad_pre1 = join(sums, parts, mask=pre1)

    gathered = gather_pieces(grad_pre1, "feat")
    keep, send = small_call(
        functools.partial(first_kernel, scale, cuts),
        [grads, grads],
        [seconds, *held, *grad_pre1],
        flops,
    )
    addends = dom_sums(keep, send)
    own, *sends = layer(tiles, gathered, weight1, blocks, slots)
    sums = boundary(own, sends)
    block = jax.ShapeDtypeStruct((width, width), jnp.bfloat16)
    total, *back = small_call(parted_kernel, [grads, *[block] * count], addends)
    back = [exchanged(back[m], "feat", lambda s, m=m: s ^ m) for m in range(1, count)]
    wide = jax.ShapeDtypeStruct((width, count * width), jnp.bfloat16)
    grad = small_call(placed_kernel, wide, [total, *back])
    other = exchanged(grad, "dom", lambda s: s ^ 1)
    wide = jax.ShapeDtypeStruct(wide.shape, jnp.float32)
    outs = [wide, wide, jax.ShapeDtypeStruct((nodes, width), jnp.bfloat16)]
    second, first, grad_input = join(sums, outs, extra=[grad, other])
    return (second, first, grad_input)


def layer(tiles, gathered, weight, blocks, slots):
    total = None
    for part, pieces in zip(tiles, gathered):
        total, *sends = spread(part, pieces, weight, blocks, slots, total)
    return total, *sends


def solution(mesh):
    in_specs = (
        P("dom", "feat"),
        P("dom", "feat"),
        P("feat", None),
        P("dom", "feat"),
        P("dom", "feat"),
        P("feat", None),
        P("dom", None, None, None),
        P("dom", None),
    )
    out_specs = (P("feat", None), P("feat", None), P("dom", "feat"))
    return jax.shard_map(shards, mesh=mesh, in_specs=in_specs, out_specs=out_specs, check_vma=False)
```

```python
import functools
import math

import jax
import jax.numpy as jnp
from jax import lax
from jax.experimental import pallas as pl
from jax.experimental.pallas import tpu as pltpu
from jax.sharding import PartitionSpec as P


VMEM = pl.BlockSpec(memory_space=pltpu.VMEM)
ANY = pl.BlockSpec(memory_space=pl.ANY)
SMEM = pl.BlockSpec(memory_space=pltpu.SMEM)


def exchanged(value, axis, partner):
    count = lax.axis_size(axis)
    pairs = [(s, partner(s)) for s in range(count) if 0 <= partner(s) < count]
    return lax.ppermute(value, axis, pairs)


SWAPS = [
    lambda s: ((s + 1) ^ 1) - 1,
    lambda s: s ^ 1,
    lambda s: ((s + 2) ^ 2) - 2,
    lambda s: s ^ 2,
]


def after(value, *earlier):
    return lax.optimization_barrier((value, *earlier))[0]


def gather_pieces(chunks, axis, earlier=()):
    held = [{0: chunk} for chunk in chunks]
    mask = lax.axis_size(axis) // 2
    first = True
    while mask:
        moves = [list(pieces) for pieces in held]
        for step in range(len(moves[0])):
            for c, (pieces, move) in enumerate(zip(held, moves)):
                m = move[step]
                got = exchanged(pieces[m], axis, lambda s, mask=mask: s ^ mask)
                pieces[m | mask] = after(got, *earlier) if first and earlier and c == 0 else got
        first = False
        mask //= 2
    return [[pieces[m] for m in sorted(pieces)] for pieces in held]


def prepare_kernel(targets_hbm, blocks_hbm, *refs):
    count = (len(refs) - 5) // 2
    weight_refs, slots_ref, blocks_ref = refs[:count], refs[count], refs[count + 1]
    outs, (targets_ref, target_sem, block_sem) = refs[count + 2 : -3], refs[-3:]
    block_copy = pltpu.make_async_copy(blocks_hbm, blocks_ref, block_sem)
    target_copy = pltpu.make_async_copy(targets_hbm, targets_ref, target_sem)
    block_copy.start()
    target_copy.start()
    place = lax.axis_index("feat")
    for weight_ref, out in zip(weight_refs, outs):
        width, total = weight_ref.shape
        for m in range(total // width):
            start = pl.multiple_of((place ^ m) * width, width)
            out[m * width : (m + 1) * width, :] = weight_ref[:, pl.ds(start, width)].T
    tile_count, entries = slots_ref.shape
    half = tile_count // 2
    index = lax.axis_index("dom")
    odd, upper = index & 1, (index & 2) // 2
    target_copy.wait()

    def body(r, carry):
        for k in range(entries):
            target = targets_ref[r, k]
            part = lax.div(target, jnp.int32(tile_count))
            offset = part - index
            within = target - part * tile_count
            up = offset > 0
            near = jnp.where(up, 1 - odd, odd)
            far = 2 + jnp.where(up, 1 - upper, upper)
            swap = jnp.where(jnp.abs(offset) == 1, near, far)
            outer = tile_count + swap * half + jnp.where(up, within, within - half)
            slots_ref[r, k] = jnp.where(offset == 0, within, outer)
        return carry

    lax.fori_loop(0, tile_count, body, 0)
    block_copy.wait()


def prepare(targets, blocks, weights):
    outs = [
        jax.ShapeDtypeStruct(targets.shape, jnp.int32),
        jax.ShapeDtypeStruct(blocks.shape, blocks.dtype),
    ]
    outs += [jax.ShapeDtypeStruct(w.shape[::-1], w.dtype) for w in weights]
    return pl.pallas_call(
        prepare_kernel,
        out_shape=outs,
        in_specs=[ANY, pl.BlockSpec(memory_space=pltpu.HBM)] + [VMEM] * len(weights),
        out_specs=[SMEM] + [VMEM] * (len(outs) - 1),
        scratch_shapes=[
            pltpu.SMEM(targets.shape, jnp.int32),
            pltpu.SemaphoreType.DMA,
            pltpu.SemaphoreType.DMA,
        ],
        compiler_params=pltpu.CompilerParams(vmem_limit_bytes=8 << 20),
        cost_estimate=pl.CostEstimate(flops=0, bytes_accessed=4 * blocks.size, transcendentals=0),
        name="prepare",
    )(targets, blocks, *weights)


def unrolling(count):
    return max(n for n in range(1, 7) if count % n == 0)


def spread_kernel(first, tiles, slots_ref, weights, blocks, *refs):
    last = tiles[1] == blocks.shape[0]
    width = weights.shape[1]
    pieces = weights.shape[0] // width
    piece_refs, refs = refs[:pieces], refs[pieces:]
    total, sends, values = refs[0 if first else 1], refs[1 if first else 2 : -1], refs[-1]
    tile_count, count, size, _ = blocks.shape
    if first:
        total[...] = jnp.zeros_like(total)
    group = 2
    for i in range((tiles[1] - tiles[0]) // group):
        rows = slice(i * group * size, (i + 1) * group * size)
        left = jnp.concatenate([piece[rows, :] for piece in piece_refs], axis=1)
        value = jnp.dot(left, weights[...], preferred_element_type=jnp.float32)
        value = value.astype(values.dtype).reshape(group, size, width)
        values[i * group : (i + 1) * group] = value

    def body(i, carry):
        value = values[i]
        r = tiles[0] + i
        for k in range(count):
            slot = slots_ref[r, k]
            total[slot] += jnp.dot(blocks[r, k], value, preferred_element_type=jnp.float32)
        return carry

    lax.fori_loop(0, tiles[1] - tiles[0], body, 0, unroll=unrolling(tiles[1] - tiles[0]))
    half = tile_count // 2
    for n, send in enumerate(sends if last else ()):
        start = tile_count + n * half
        send[...] = total[start : start + half].astype(send.dtype)


def spread(tiles, pieces, weight, blocks, slots, total=None):
    tile_count, count, size, _ = blocks.shape
    half = tile_count // 2
    width = weight.shape[1]
    held = tiles[1] - tiles[0]
    outs = [
        jax.ShapeDtypeStruct((tile_count + len(SWAPS) * half, size, width), jnp.float32)
    ]
    if tiles[1] == tile_count:
        outs += [jax.ShapeDtypeStruct((half, size, width), jnp.bfloat16)] * len(SWAPS)
    args = [slots, weight, blocks, *pieces]
    aliases = {}
    if total is not None:
        aliases[len(args)] = 0
        args.append(total)
    return pl.pallas_call(
        functools.partial(spread_kernel, total is None, tiles),
        out_shape=outs,
        in_specs=[SMEM] + [VMEM] * (len(args) - 1),
        out_specs=[VMEM] * len(outs),
        input_output_aliases=aliases,
        scratch_shapes=[pltpu.VMEM((held, size, width), jnp.bfloat16)],
        cost_estimate=pl.CostEstimate(
            flops=2 * held * size * width * (count * size + weight.shape[0]),
            bytes_accessed=held * size * width * 2 * (count + 8),
            transcendentals=0,
        ),
        compiler_params=pltpu.CompilerParams(vmem_limit_bytes=16 << 20),
        name="spread",
    )(*args)


def join_kernel(masked, tile_count, own, next_over, across, next_apart, apart, *refs):
    size = own.shape[1]
    half = tile_count // 2
    index = lax.axis_index("dom")
    odd, upper = (index & 1) == 1, (index & 2) == 2
    if masked:
        mask, *outs = refs
    else:
        grad, other, *results, second, first, out, sems = refs
        outs = [out]

        @pl.when(odd)
        def _():
            second[...] = grad[...].astype(second.dtype)
            first[...] = other[...].astype(first.dtype)

        @pl.when(jnp.logical_not(odd))
        def _():
            second[...] = other[...].astype(second.dtype)
            first[...] = grad[...].astype(first.dtype)

        quarter = out.shape[0] // 4
        copies = [
            pltpu.make_async_copy(second, results[0], sems.at[0]),
            pltpu.make_async_copy(first, results[1], sems.at[1]),
        ]
        for n in range(4):
            rows = pl.ds(n * quarter, quarter)
            copies.append(
                pltpu.make_async_copy(out.at[rows], results[2].at[rows], sems.at[2 + n])
            )
        copies[0].start()
        copies[1].start()

    places = [(out, i) for out in outs for i in range(out.shape[0] // size)]

    def write(tile, near, far):
        total = own[tile]
        total += near[tile % half].astype(jnp.float32) + far[tile % half].astype(jnp.float32)
        if masked:
            total = jnp.where(mask[tile * size : (tile + 1) * size, :] > 0, total, 0.0)
        out, i = places[tile]
        out[i * size : (i + 1) * size, :] = total.astype(out.dtype)

    for is_odd in (False, True):
        for is_upper in (False, True):

            @pl.when((odd == is_odd) & (upper == is_upper))
            def _(is_odd=is_odd, is_upper=is_upper):
                near = [across, next_over] if is_odd else [next_over, across]
                far = [apart, next_apart] if is_upper else [next_apart, apart]
                for tile in range(tile_count):
                    write(tile, near[tile // half], far[tile // half])
                    if not masked and (tile + 1) % (tile_count // 4) == 0:
                        copies[2 + tile // (tile_count // 4)].start()

    for copy in () if masked else copies:
        copy.wait()


def boundary(own, sends):
    got = [exchanged(send, "dom", swap) for send, swap in zip(sends, SWAPS)]
    return own, *got


def join(sums, outs, mask=None, extra=()):
    masked = mask is not None
    args = [*sums, mask] if masked else [*sums, *extra]
    return pl.pallas_call(
        functools.partial(join_kernel, masked, 2 * sums[1].shape[0]),
        out_shape=outs,
        in_specs=[VMEM] * len(args),
        out_specs=[VMEM if masked else ANY] * len(outs),
        scratch_shapes=[]
        if masked
        else [*(pltpu.VMEM(o.shape, o.dtype) for o in outs), pltpu.SemaphoreType.DMA((6,))],
        compiler_params=pltpu.CompilerParams(vmem_limit_bytes=8 << 20),
        cost_estimate=pl.CostEstimate(
            flops=0, bytes_accessed=12 * sums[1].size, transcendentals=0
        ),
        name="join",
    )(*args)


def term(left, right):
    return lax.dot_general(left, right, (((0,), (0,)), ((), ())), preferred_element_type=jnp.float32)


def second_kernel(scale, cuts, agg, *refs):
    *chunks, out = refs
    count = len(chunks) // len(cuts)
    for m in range(count):
        total = None
        for c, (first, last) in enumerate(cuts):
            part = term(agg[first:last, :], chunks[c * count + m][...])
            total = part if total is None else total + part
        out[m] = (total * scale).astype(out.dtype)


def first_kernel(scale, cuts, seconds, *refs):
    count = seconds.shape[0]
    pieces, chunks, (keep, send) = refs[:count], refs[count:-2], refs[-2:]
    odd = (lax.axis_index("dom") & 1) == 1
    for m in range(count):
        total = None
        for (first, last), chunk in zip(cuts, chunks):
            part = term(pieces[m][first:last, :], chunk[...])
            total = part if total is None else total + part
        total = (total * scale).astype(send.dtype)
        keep[m] = jnp.where(odd, seconds[m], total)
        send[m] = jnp.where(odd, total, seconds[m])


def parted_kernel(value, other, total, *blocks):
    for m, block in enumerate(blocks):
        sums = value[m].astype(jnp.float32) + other[m].astype(jnp.float32)
        total[m] = sums.astype(total.dtype)
        block[...] = total[m]


def placed_kernel(total, *refs):
    *blocks, out = refs
    odd = (lax.axis_index("dom") & 1) == 1
    place = lax.axis_index("feat")
    width = out.shape[0]
    for m in range(total.shape[0]):
        columns = pl.ds(pl.multiple_of((place ^ m) * width, width), width)
        out[:, columns] = jnp.where(odd, total[m], blocks[m - 1][...] if m else total[m])


def small_call(kernel, outs, args, flops=0):
    return pl.pallas_call(
        kernel,
        out_shape=outs,
        in_specs=[VMEM] * len(args),
        out_specs=jax.tree.map(lambda _: VMEM, outs),
        cost_estimate=pl.CostEstimate(
            flops=flops, bytes_accessed=sum(2 * a.size for a in args), transcendentals=0
        ),
        compiler_params=pltpu.CompilerParams(vmem_limit_bytes=8 << 20),
    )(*args)


def added(value, other):
    return (value.astype(jnp.float32) + other.astype(jnp.float32)).astype(jnp.bfloat16)


def dom_sums(keep, send):
    value, other = keep, exchanged(send, "dom", lambda s: s ^ 1)
    mask = lax.axis_size("dom") // 2
    while mask > 1:
        value = added(value, other)
        other = exchanged(value, "dom", lambda s, mask=mask: s ^ mask)
        mask //= 2
    return value, other


def shards(grad_pre2, aggregated2, weight2, pre1, aggregated1, weight1, blocks, targets):
    nodes, width = grad_pre2.shape
    scale = 1.0 / math.sqrt(nodes * lax.axis_size("dom"))
    tile_count, _, size, _ = blocks.shape
    cut = tile_count * 5 // 8
    tiles = [(0, cut), (cut, tile_count)]
    cuts = [(t[0] * size, t[1] * size) for t in tiles]
    parts = [jax.ShapeDtypeStruct((r[1] - r[0], width), jnp.bfloat16) for r in cuts]
    slots, blocks, weight2, weight1 = prepare(targets, blocks, [weight2, weight1])

    chunks = [grad_pre2[: cuts[0][1]], lax.optimization_barrier(grad_pre2)[cuts[0][1] :]]
    gathered = gather_pieces(chunks, "feat", [weight2])
    count = len(gathered[0])
    flops = 2 * nodes * count * width**2
    grads = jax.ShapeDtypeStruct((count, width, width), jnp.bfloat16)
    own, *sends = layer(tiles, gathered, weight2, blocks, slots)
    sums = boundary(own, sends)
    (held,) = gather_pieces([aggregated1], "feat")
    seconds = small_call(
        functools.partial(second_kernel, scale, cuts),
        grads,
        [after(aggregated2, sends[0]), *gathered[0], *gathered[1]],
        flops,
    )
    grad_pre1 = join(sums, parts, mask=pre1)

    gathered = gather_pieces(grad_pre1, "feat")
    keep, send = small_call(
        functools.partial(first_kernel, scale, cuts),
        [grads, grads],
        [seconds, *held, *grad_pre1],
        flops,
    )
    addends = dom_sums(keep, send)
    own, *sends = layer(tiles, gathered, weight1, blocks, slots)
    sums = boundary(own, sends)
    block = jax.ShapeDtypeStruct((width, width), jnp.bfloat16)
    total, *back = small_call(parted_kernel, [grads, *[block] * count], addends)
    back = [exchanged(back[m], "feat", lambda s, m=m: s ^ m) for m in range(1, count)]
    wide = jax.ShapeDtypeStruct((width, count * width), jnp.bfloat16)
    grad = small_call(placed_kernel, wide, [total, *back])
    other = exchanged(grad, "dom", lambda s: s ^ 1)
    wide = jax.ShapeDtypeStruct(wide.shape, jnp.float32)
    outs = [wide, wide, jax.ShapeDtypeStruct((nodes, width), jnp.bfloat16)]
    second, first, grad_input = join(sums, outs, extra=[grad, other])
    return (second, first, grad_input)


def layer(tiles, gathered, weight, blocks, slots):
    total = None
    for part, pieces in zip(tiles, gathered):
        total, *sends = spread(part, pieces, weight, blocks, slots, total)
    return total, *sends


def solution(mesh):
    in_specs = (
        P("dom", "feat"),
        P("dom", "feat"),
        P("feat", None),
        P("dom", "feat"),
        P("dom", "feat"),
        P("feat", None),
        P("dom", None, None, None),
        P("dom", None),
    )
    out_specs = (P("feat", None), P("feat", None), P("dom", "feat"))
    return jax.shard_map(shards, mesh=mesh, in_specs=in_specs, out_specs=out_specs, check_vma=False)
```
